128 devices in a mesh: shard: 2 (over y_lo), context: 16 (over x, y_hi, core), tensor: 4 (over z).
Axes of the slice: x: 4, y: 4 (y_hi: 2, y_lo: 2; y = y_hi * 2 + y_lo), z: 4, core: 2. Of those that a mesh axis runs over, the one named last changes fastest.
Arguments:
- layer_input_residual: float32 [2, 6144, 768], P('shard', 'context'), may hold values from -6 to 6
- positions: int32 [2, 6144], P('shard'), may hold values from 0 to 6143, as said below
- ln1_gain: bfloat16 [768], P(('shard', 'context')), may hold values from 0.5 to 1.5
- ln1_bias: bfloat16 [768], P(('shard', 'context')), may hold values from -3 to 3
- ln2_gain: bfloat16 [768], P(('shard', 'context')), may hold values from 0.3984375 to 2.5
- ln2_bias: bfloat16 [768], P(('shard', 'context')), may hold values from -3 to 3
- w_qkv: bfloat16 [768, 3, 768], P(('shard', 'context'), None, 'tensor'), may hold values from -0.21875 to 0.21875
- query_key_value_bias: float32 [3, 768], P(None, 'tensor'), may hold values from -9 to 9
- w_out: bfloat16 [768, 768], P(('shard', 'context'), 'tensor'), may hold values from -0.4375 to 0.4375
- b_out: bfloat16 [768], P(('shard', 'context')), may hold values from -3 to 3
- w_up: bfloat16 [768, 3072], P(('shard', 'context'), 'tensor'), may hold values from -0.21875 to 0.21875
- up_bias_vector: float32 [3072], P('tensor'), may hold values from -3 to 3
- w_down: bfloat16 [768, 3072], P(('shard', 'context'), 'tensor'), may hold values from -0.109375 to 0.109375
- b_down: bfloat16 [768], P(('shard', 'context')), may hold values from -3 to 3
- grad_out: float32 [2, 6144, 768], P('shard', 'context'), may hold values from -6 to 6
Outputs:
- layer_out: float32 [2, 6144, 768], P('shard', 'context')
- grad_in: float32 [2, 6144, 768], P('shard', 'context')
- g_ln1_gain: float32 [768], P(('shard', 'context'))
- g_ln1_bias: float32 [768], P(('shard', 'context'))
- g_ln2_gain: float32 [768], P(('shard', 'context'))
- g_ln2_bias: float32 [768], P(('shard', 'context'))
- query_key_value_weight_gradient: float32 [768, 3, 768], P(('shard', 'context'), None, 'tensor')
- g_b_qkv: float32 [3, 768], P(None, 'tensor')
- out_weight_gradient: float32 [768, 768], P(('shard', 'context'), 'tensor')
- g_b_out: float32 [768], P(('shard', 'context'))
- up_weight_gradient: float32 [768, 3072], P(('shard', 'context'), 'tensor')
- g_b_up: float32 [3072], P('tensor')
- down_weight_gradient: float32 [768, 3072], P(('shard', 'context'), 'tensor')
- g_b_down: float32 [768], P(('shard', 'context'))
The draws below stay inside these ranges and needn't reach their ends.
Inputs may be any that keep to these rules, and one draw needn't show every extreme that they name: Each row of positions is a permutation of the positions of one sequence, made of runs of 192 consecutive positions, each run starting at a multiple of 192.
All inputs are finite; a program needn't handle non-finite values.
Results may differ from the reference program's by a relative error of at most 0.029.
The reference program's roundings to bfloat16 on the way count: a program that leaves them out, or rounds other values in their place, can miss the bound.
Values may be sent and summed in bfloat16 or wider, within the bound.
A program may use at most 128 MiB of HBM per device.

```python
import math
import jax
import jax.numpy as jnp
from jax import lax

D = 768
HEADS = 12
HS = 64
ROT = 16
FF = 3072
INNER = 768
LEN = 6144
SEQS = 2
BLK = 192


def draw_positions(key, part):
    run_count = LEN // BLK
    seq_keys = jax.random.split(key, SEQS)
    orders = jax.vmap(lambda one_key: jax.random.permutation(one_key, run_count))(seq_keys)
    within = jnp.arange(BLK, dtype=jnp.int32)
    layout = orders.astype(jnp.int32)[:, :, None] * BLK + within[None, None, :]
    return layout.reshape(SEQS, LEN).astype(jnp.int32)


def draw_query_key_value_bias(key, part):
    key_base = jax.random.fold_in(key, 11)
    base = 0.3 * jnp.clip(jax.random.normal(key_base, (3, INNER), jnp.float32), -8.0, 8.0)
    return base.astype(jnp.float32)


def level_of(rng, extent, cuts, smallest, largest):
    factor_of, own = 1.0, jax.random.fold_in(rng, 6)
    for position, shards_of in cuts:
        steps = jnp.exp(jax.random.uniform(jax.random.fold_in(own, position), (shards_of,), jnp.float32, smallest / len(cuts), largest / len(cuts)))
        factor_of = factor_of * jnp.repeat(steps, extent[position] // shards_of).reshape([-1 if axis == position else 1 for axis in range(len(extent))])
    return factor_of


def normal_values(own_key, shape, deviation, limit, cuts=(), held_as=jnp.bfloat16):
    array = jax.random.normal(own_key, shape, jnp.float32) * deviation
    if len(cuts) > 0:
        array = level_of(own_key, shape, cuts, -0.22, 0.18) * array
    return jnp.clip(array, min=-limit, max=limit).astype(held_as)


def setup_inputs(seed: int = 0) -> dict:
    seeds = jax.random.split(jax.random.key(seed), 16)
    return {
        "layer_input_residual": normal_values(seeds[0], (SEQS, LEN, D), 1.0, 6.0, ((0, 2), (1, 16)), jnp.float32),
        "positions": draw_positions(jax.random.fold_in(seeds[15], 71), 0),
        "ln1_gain": jnp.clip(1.0 + 0.1 * jax.random.normal(seeds[2], (D,), jnp.float32), 0.5, 1.5).astype(jnp.bfloat16),
        "ln1_bias": normal_values(seeds[3], (D,), 0.5, 3.0, ((0, 32),)),
        "ln2_gain": jnp.clip(jnp.exp(math.log(2.5) - 1.8364954 * jax.random.uniform(seeds[4], (D,), jnp.float32) ** level_of(seeds[4], (D,), ((0, 32),), -0.2, 0.2)), 0.3984375, 2.5).astype(jnp.bfloat16),
        "ln2_bias": normal_values(seeds[5], (D,), 0.5, 3.0, ((0, 32),)),
        "w_qkv": normal_values(seeds[6], (D, 3, INNER), D ** -0.5, 0.21875, ((0, 32), (2, 4))),
        "query_key_value_bias": draw_query_key_value_bias(jax.random.fold_in(seeds[15], 71), 0),
        "w_out": normal_values(seeds[8], (D, INNER), (INNER // 4) ** -0.5, 0.4375, ((0, 32), (1, 4))),
        "b_out": normal_values(seeds[9], (D,), 0.5, 3.0, ((0, 32),)),
        "w_up": normal_values(seeds[10], (D, FF), D ** -0.5, 0.21875, ((0, 32), (1, 4))),
        "up_bias_vector": normal_values(seeds[11], (FF,), 0.5, 3.0, ((0, 4),), jnp.float32),
        "w_down": normal_values(seeds[12], (D, FF), FF ** -0.5, 0.109375, ((0, 32), (1, 4))),
        "b_down": normal_values(seeds[13], (D,), 0.5, 3.0, ((0, 32),)),
        "grad_out": normal_values(seeds[14], (SEQS, LEN, D), 1.0, 6.0, ((0, 2), (1, 16)), jnp.float32),
    }


norm_eps = 1e-05

def layer_norm_forward(values):
    centered = values - lax.optimization_barrier(jnp.mean(values, axis=-1, keepdims=True))
    inverse_deviation = lax.rsqrt(lax.optimization_barrier(jnp.mean(centered * centered, axis=-1, keepdims=True)) + norm_eps)
    return (centered * inverse_deviation, inverse_deviation)

def rotary_tables(pos_rows):
    half_rot = ROT // 2
    freqs = jnp.exp(-(jnp.arange(half_rot).astype(jnp.float32) * (2.0 / ROT)) * math.log(10000.0))
    angles = pos_rows.astype(jnp.float32)[..., None] * freqs
    return (jnp.cos(angles), jnp.sin(angles))

def rotate_heads(tensor, cosine, sine, sign_dir):
    half_rot = ROT // 2
    first = tensor[..., :half_rot]
    second = tensor[..., half_rot:ROT]
    cos_b = cosine[..., None, :]
    sin_b = sine[..., None, :] * sign_dir
    return jnp.concatenate([first * cos_b - second * sin_b, second * cos_b + first * sin_b, tensor[..., ROT:]], axis=-1)

def gelu_slope(pre_act):
    cdf_val = 0.5 * (1.0 + jax.scipy.special.erf(pre_act * 0.7071067811865476))
    pdf_val = jnp.exp(-0.5 * pre_act * pre_act) * 0.3989422804014327
    return cdf_val + pre_act * pdf_val

def layer_norm_backward(norm_output_gradient, centered_scaled_input, inverse_deviation, gain_vector_rows):
    incoming_gradient = norm_output_gradient * gain_vector_rows
    input_gradient_piece = inverse_deviation * (incoming_gradient - lax.optimization_barrier(jnp.mean(incoming_gradient, axis=-1, keepdims=True)) - centered_scaled_input * lax.optimization_barrier(jnp.mean(incoming_gradient * centered_scaled_input, axis=-1, keepdims=True)))
    return (input_gradient_piece, lax.optimization_barrier(jnp.sum(norm_output_gradient * centered_scaled_input, axis=0)), lax.optimization_barrier(jnp.sum(norm_output_gradient, axis=0)))

def reference(layer_input_residual, positions, ln1_gain, ln1_bias, ln2_gain, ln2_bias, w_qkv, query_key_value_bias, w_out, b_out, w_up, up_bias_vector, w_down, b_down, grad_out):
    scale = HS ** (-0.5)
    qblock = math.gcd(512, LEN)
    nblocks = LEN // qblock
    first_norm_gain = ln1_gain.astype(jnp.float32)
    second_norm_gain = ln2_gain.astype(jnp.float32)
    first_norm_bias = ln1_bias.astype(jnp.float32)
    second_norm_bias = ln2_bias.astype(jnp.float32)
    bias_sum = b_out.astype(jnp.float32) + b_down.astype(jnp.float32)
    query_key_value_weight_single = w_qkv.astype(jnp.float32)

    def one_sequence(totals, items):
        sequence_input, pos_seq, g_seq = items
        centered_scaled_input, inverse_deviation = layer_norm_forward(sequence_input)
        first_norm_output = (centered_scaled_input * first_norm_gain + first_norm_bias).astype(jnp.bfloat16)
        second_norm_output = (centered_scaled_input * second_norm_gain + second_norm_bias).astype(jnp.bfloat16)
        attention_projected = jnp.einsum('bm,mjp->bjp', first_norm_output.astype(jnp.float32), query_key_value_weight_single) + query_key_value_bias
        cosine, sine = rotary_tables(pos_seq)
        query = rotate_heads(attention_projected[:, 0].reshape(LEN, HEADS, HS), cosine, sine, 1.0).astype(jnp.bfloat16)
        keys = rotate_heads(attention_projected[:, 1].reshape(LEN, HEADS, HS), cosine, sine, 1.0).astype(jnp.bfloat16)
        values = attention_projected[:, 2].reshape(LEN, HEADS, HS).astype(jnp.bfloat16)
        keys_f = keys.astype(jnp.float32)
        values_f = values.astype(jnp.float32)

        def scores_for(block_idx):
            start = block_idx * qblock
            query_blk = lax.dynamic_slice_in_dim(query, start, qblock, 0).astype(jnp.float32)
            query_pos = lax.dynamic_slice_in_dim(pos_seq, start, qblock, 0)
            scores = jnp.einsum('qhd,khd->hqk', query_blk, keys_f) * scale
            allowed = pos_seq[None, None, :] <= query_pos[None, :, None]
            return (scores, allowed, query_blk)

        def forward_block(block_idx):
            scores, allowed, query_blk = scores_for(block_idx)
            masked = jnp.where(allowed, scores, -jnp.inf)
            row_max = lax.optimization_barrier(jnp.max(masked, axis=-1, keepdims=True))
            log_norm = row_max + jnp.log(lax.optimization_barrier(jnp.sum(jnp.exp(masked - row_max), axis=-1, keepdims=True)))
            weights_full = jnp.where(allowed, jnp.exp(scores - log_norm), 0.0)
            out_blk = jnp.einsum('hqk,khd->qhd', weights_full, values_f, precision=lax.Precision.HIGHEST)
            return (out_blk.astype(jnp.bfloat16), log_norm[..., 0])
        block_ids = jnp.arange(nblocks).astype(jnp.int32)
        att_blocks, norm_blocks = lax.map(forward_block, block_ids)
        attended = att_blocks.reshape(LEN, HEADS, HS)
        attention_rows_flat = attended.reshape(LEN, INNER)
        attn_proj = jnp.dot(attention_rows_flat, w_out.T, preferred_element_type=jnp.float32)
        pre_act = jnp.dot(second_norm_output, w_up, preferred_element_type=jnp.float32) + up_bias_vector
        gelu_output = jax.nn.gelu(pre_act, approximate=False).astype(jnp.bfloat16)
        mlp_proj = jnp.dot(gelu_output, w_down.T, preferred_element_type=jnp.float32)
        y_seq = sequence_input + (attn_proj + mlp_proj) + bias_sum
        gradient_half_precision = g_seq.astype(jnp.bfloat16)
        g_vec_out = lax.optimization_barrier(jnp.sum(g_seq, axis=0))
        down_weight_gradient = jnp.dot(gradient_half_precision.T, gelu_output, preferred_element_type=jnp.float32)
        gelu_gradient = jnp.dot(gradient_half_precision, w_down, preferred_element_type=jnp.float32)
        g_pre = gelu_gradient * gelu_slope(pre_act)
        g_b_up = lax.optimization_barrier(jnp.sum(g_pre, axis=0))
        preact_gradient_half = g_pre.astype(jnp.bfloat16)
        up_weight_gradient = jnp.dot(second_norm_output.T, preact_gradient_half, preferred_element_type=jnp.float32)
        norm2_output_gradient = jnp.dot(preact_gradient_half, w_up.T, preferred_element_type=jnp.float32)
        out_weight_gradient = jnp.dot(gradient_half_precision.T, attention_rows_flat, preferred_element_type=jnp.float32)
        g_attended = jnp.dot(gradient_half_precision, w_out, preferred_element_type=jnp.float32).astype(jnp.bfloat16).reshape(LEN, HEADS, HS)
        row_delta = lax.optimization_barrier(jnp.sum(g_attended.astype(jnp.float32) * attended.astype(jnp.float32), axis=-1))

        def backward_block(carry, inputs):
            grad_key, grad_val = carry
            block_idx, log_norm = inputs
            scores, allowed, query_blk = scores_for(block_idx)
            start = block_idx * qblock
            g_att_blk = lax.dynamic_slice_in_dim(g_attended, start, qblock, 0).astype(jnp.float32)
            delta_blk = lax.dynamic_slice_in_dim(row_delta, start, qblock, 0).T
            attn_weights = jnp.where(allowed, jnp.exp(scores - log_norm[..., None]), 0.0)
            weights_bf = attn_weights.astype(jnp.bfloat16).astype(jnp.float32)
            grad_val = grad_val + jnp.einsum('hqk,qhd->khd', weights_bf, g_att_blk)
            g_prob = jnp.einsum('qhd,khd->hqk', g_att_blk, values_f)
            g_scores = (attn_weights * (g_prob - delta_blk[..., None]) * scale).astype(jnp.bfloat16).astype(jnp.float32)
            grad_q_blk = jnp.einsum('hqk,khd->qhd', g_scores, keys_f)
            grad_key = grad_key + jnp.einsum('hqk,qhd->khd', g_scores, query_blk)
            return ((grad_key, grad_val), grad_q_blk)
        zero_kv = jnp.zeros((LEN, HEADS, HS), jnp.float32)
        (grad_key, grad_val), grad_q_blocks = lax.scan(backward_block, (zero_kv, zero_kv), (block_ids, norm_blocks))
        g_query = rotate_heads(grad_q_blocks.reshape(LEN, HEADS, HS), cosine, sine, -1.0)
        g_keys = rotate_heads(grad_key, cosine, sine, -1.0)
        g_projected = jnp.stack([g_query.reshape(LEN, INNER), g_keys.reshape(LEN, INNER), grad_val.reshape(LEN, INNER)], axis=1)
        g_b_qkv = lax.optimization_barrier(jnp.sum(g_projected, axis=0))
        projection_gradient_half = g_projected.astype(jnp.bfloat16).astype(jnp.float32)
        query_key_value_weight_gradient = jnp.einsum('bn,bxm->nxm', first_norm_output.astype(jnp.float32), projection_gradient_half)
        norm1_output_gradient = jnp.einsum('wmr,omr->wo', projection_gradient_half, query_key_value_weight_single)
        input_gradient_first, first_gain_gradient, first_bias_gradient = layer_norm_backward(norm1_output_gradient, centered_scaled_input, inverse_deviation, first_norm_gain)
        input_gradient_second, second_gain_gradient, second_bias_gradient = layer_norm_backward(norm2_output_gradient, centered_scaled_input, inverse_deviation, second_norm_gain)
        dx_seq = g_seq + (input_gradient_first + input_gradient_second)
        vec_grads = jnp.stack([first_gain_gradient, first_bias_gradient, second_gain_gradient, second_bias_gradient, g_vec_out], axis=0)
        new_totals = (totals[0] + query_key_value_weight_gradient, totals[1] + out_weight_gradient, totals[2] + up_weight_gradient, totals[3] + down_weight_gradient, totals[4] + g_b_qkv, totals[5] + g_b_up, totals[6] + vec_grads)
        return (new_totals, (y_seq, dx_seq))
    init_totals = (jnp.zeros((D, 3, INNER), jnp.float32), jnp.zeros((D, INNER), jnp.float32), jnp.zeros((D, FF), jnp.float32), jnp.zeros((D, FF), jnp.float32), jnp.zeros((3, INNER), jnp.float32), jnp.zeros((FF,), jnp.float32), jnp.zeros((5, D), jnp.float32))
    totals, (layer_out, grad_in) = lax.scan(one_sequence, init_totals, (layer_input_residual, positions, grad_out))
    vec_grads = totals[6]
    return (layer_out, grad_in, vec_grads[0], vec_grads[1], vec_grads[2], vec_grads[3], totals[0], totals[4], totals[1], vec_grads[4], totals[2], totals[5], totals[3], vec_grads[4])
```

```python
import functools
import math

import jax
import jax.numpy as jnp
from jax import lax
from jax.experimental import pallas as pl
from jax.experimental.pallas import tpu as pltpu
from jax.sharding import PartitionSpec as P

HS = 64
ROT = 16
BF = jnp.bfloat16
F32 = jnp.float32
MESH = pl.DeviceIdType.MESH
norm_eps = 1e-05


def coords():
    s = lax.axis_index("shard")
    c = lax.axis_index("context")
    z = lax.axis_index("tensor")
    x = lax.div(c, 4)
    yh = lax.rem(lax.div(c, 2), 2)
    k = lax.rem(c, 2)
    return x, yh * 2 + s, k, z


def dev(x, y, k, z):
    return (lax.rem(y, 2), x * 4 + lax.div(y, 2) * 2 + k, z)


def m4(a):
    return lax.rem(a, 4)


class Mail:
    def __init__(self, send_sems, recv_sems):
        self.send_sems, self.recv_sems, self.made = send_sems, recv_sems, []

    def send(self, src, dst, device):
        i = len(self.made)
        assert i < self.send_sems.shape[0]
        copy = pltpu.make_async_remote_copy(
            src_ref=src,
            dst_ref=dst,
            send_sem=self.send_sems.at[i],
            recv_sem=self.recv_sems.at[i],
            device_id=device,
            device_id_type=MESH,
        )
        copy.start()
        self.made.append(copy)
        return i

    def recv(self, i):
        self.made[i].wait_recv()

    def close(self):
        for copy in self.made:
            copy.wait_send()


def greet(devices):
    barrier = pltpu.get_barrier_semaphore()
    for device in devices:
        pl.semaphore_signal(barrier, inc=1, device_id=device, device_id_type=MESH)
    pl.semaphore_wait(barrier, len(devices))


def comm_call(kernel, name, cid, n_copies, outs, scratch, args, in_vmem=None, out_vmem=None):
    anyspec = pl.BlockSpec(memory_space=pl.ANY)
    vspec = pl.BlockSpec(memory_space=pltpu.VMEM)
    in_vmem = in_vmem or [False] * len(args)
    out_vmem = out_vmem or [False] * len(outs)
    return pl.pallas_call(
        kernel,
        name=name,
        out_shape=[jax.ShapeDtypeStruct(*o) for o in outs],
        in_specs=[vspec if v else anyspec for v in in_vmem],
        out_specs=[vspec if v else anyspec for v in out_vmem],
        scratch_shapes=list(scratch)
        + [
            pltpu.SemaphoreType.DMA((n_copies,)),
            pltpu.SemaphoreType.DMA((n_copies,)),
            pltpu.SemaphoreType.DMA((4,)),
        ],
        compiler_params=pltpu.CompilerParams(
            collective_id=cid, has_side_effects=True, vmem_limit_bytes=56 * 1024 * 1024
        ),
    )(*args)


WCOLS = 2432
P_CUT = (0, 640, 1280)
Q_CUT = (1280, 1792, 2432)


def gather_weights_kernel(src, out, ss, rs, ls):
    x, y, k, z = coords()
    mail = Mail(ss, rs)

    def row(xx, yy):
        return lax.rem(yy, 2) * 16 + xx * 4 + lax.div(yy, 2) * 2 + k

    xs = [x, m4(x + 3), m4(x + 1), m4(x + 2)]
    ys = [y, m4(y + 3), m4(y + 1), m4(y + 2)]
    mate = dev(x, y, 1 - k, z)
    step = {
        "x": (dev(xs[2], y, k, z), dev(xs[1], y, k, z)),
        "y": (dev(x, ys[2], k, z), dev(x, ys[1], k, z)),
    }
    greet([step["x"][0], step["x"][1], step["y"][0], step["y"][1], mate])
    me = row(x, y)
    own = pltpu.make_async_copy(src, out.at[me], ls.at[0])
    own.start()

    def part(r, lo, hi):
        return out.at[r, :, pl.ds(lo, hi - lo)]

    def begin(view, r, cut, axis):
        return [
            mail.send(view, part(r, cut[0], cut[2]), step[axis][0]),
            mail.send(view, part(r, cut[0], cut[2]), step[axis][1]),
        ]

    def own_view(cut):
        return src.at[:, pl.ds(cut[0], cut[2] - cut[0])]

    mates = []

    def to_mate(r, lo, hi):
        mates.append(mail.send(part(r, lo, hi), part(r, lo, hi), mate))

    plans = [("x", "y", P_CUT), ("y", "x", Q_CUT)]
    first = [begin(own_view(cut), me, cut, a) for a, b, cut in plans]
    second = [[begin(own_view(cut), me, cut, b)] for a, b, cut in plans]
    mates.append(mail.send(src, out.at[me], mate))

    def at(a, i, j):
        return row(xs[i], ys[j]) if a == "x" else row(xs[j], ys[i])

    relays = [[], []]
    for i in (1, 2):
        for n, (a, b, cut) in enumerate(plans):
            mail.recv(first[n][i - 1])
            r = at(a, i, 0)
            lo, hi = (cut[0], cut[1]) if i == 1 else (cut[1], cut[2])
            relays[n].append(mail.send(part(r, lo, hi), part(r, lo, hi), step[a][i - 1]))
            second[n].append(begin(part(r, cut[0], cut[2]), r, cut, b))
            to_mate(r, cut[0], cut[2])
    for n, (a, b, cut) in enumerate(plans):
        for i in relays[n]:
            mail.recv(i)
        r = at(a, 3, 0)
        second[n].append(begin(part(r, cut[0], cut[2]), r, cut, b))
        to_mate(r, cut[0], cut[2])
    late = []
    for i in range(4):
        for n, (a, b, cut) in enumerate(plans):
            pair = []
            for j in (1, 2):
                mail.recv(second[n][i][j - 1])
                r = at(a, i, j)
                lo, hi = (cut[0], cut[1]) if j == 1 else (cut[1], cut[2])
                pair.append(mail.send(part(r, lo, hi), part(r, lo, hi), step[b][j - 1]))
                to_mate(r, cut[0], cut[2])
            late.append((pair, at(a, i, 3), cut))
    for pair, r, cut in late:
        for i in pair:
            mail.recv(i)
        to_mate(r, cut[0], cut[2])
    for i in mates:
        mail.recv(i)
    own.wait()
    mail.close()


def gather_weights(src):
    return comm_call(
        gather_weights_kernel, "gather_weights", 1, 80,
        [((32, 24, WCOLS), BF)], [], [src],
    )[0]


def spread_z(mail, z, x, y, k, src, dst):
    made = []
    for d in (1, 3, 2):
        peer = m4(z + d)
        made.append(mail.send(src.at[peer], dst.at[z], dev(x, y, k, peer)))
    return made


def gather_attention_kernel(a_ref, kv_ref, n2_ref, a_out, kv_out, n2_out, relay, ss, rs, ls):
    x, y, k, z = coords()
    mail = Mail(ss, rs)
    xl, xr = m4(x + 3), m4(x + 1)
    right, left = dev(xr, y, k, z), dev(xl, y, k, z)
    up, down = dev(x, m4(y + 1), k, z), dev(x, m4(y + 3), k, z)
    mate = dev(x, y, 1 - k, z)
    greet([right, left, up, down, mate] + [dev(x, y, k, m4(z + d)) for d in (1, 2, 3)])
    slot = lax.div(y, 2) * 2 + k
    far = (1 - lax.div(y, 2)) * 2 + k
    top, low = pl.ds(0, 192), pl.ds(192, 192)
    y1 = mail.send(kv_ref.at[top], relay.at[0], up)
    y2 = mail.send(kv_ref.at[low], relay.at[1], down)
    x1 = mail.send(a_ref, a_out.at[x], right)
    x2 = mail.send(a_ref, a_out.at[x], left)
    c1 = mail.send(kv_ref, kv_out.at[slot], mate)
    zs = spread_z(mail, z, x, y, k, n2_ref, n2_out)
    locals_ = [
        pltpu.make_async_copy(a_ref, a_out.at[x], ls.at[0]),
        pltpu.make_async_copy(kv_ref, kv_out.at[slot], ls.at[1]),
        pltpu.make_async_copy(n2_ref.at[z], n2_out.at[z], ls.at[2]),
    ]
    for copy in locals_:
        copy.start()
    up_slot = lax.div(m4(y + 3), 2) * 2 + k
    down_slot = lax.div(m4(y + 1), 2) * 2 + k
    mail.recv(y1)
    y3 = mail.send(relay.at[0], kv_out.at[up_slot, top], up)
    mail.recv(y2)
    y4 = mail.send(relay.at[1], kv_out.at[down_slot, low], down)
    mail.recv(x1)
    x3 = mail.send(a_out.at[xl, top], a_out.at[xl, top], right)
    mail.recv(x2)
    x4 = mail.send(a_out.at[xr, low], a_out.at[xr, low], left)
    mail.recv(y3)
    mail.recv(y4)
    c2 = mail.send(kv_out.at[far], kv_out.at[far], mate)
    for i in [x3, x4, c1, c2] + zs:
        mail.recv(i)
    for copy in locals_:
        copy.wait()
    mail.close()


def gather_attention(a, kv, n2):
    return comm_call(
        gather_attention_kernel, "gather_attention", 2, 16,
        [((4, 384, 384), BF), ((4, 384, 384), BF), ((4, 96, 768), BF)],
        [pltpu.VMEM((2, 192, 384), BF)],
        [a, kv, n2],
    )


def exchange_x(mail, x, y, k, z, src, dst, relay):
    xl, xr, xo = m4(x + 3), m4(x + 1), m4(x + 2)
    right, left = dev(xr, y, k, z), dev(xl, y, k, z)
    top, low = pl.ds(0, 96), pl.ds(96, 96)
    r1 = mail.send(src.at[xo, top], relay.at[0], right)
    r2 = mail.send(src.at[xo, low], relay.at[1], left)
    made = [
        mail.send(src.at[xr], dst.at[x], right),
        mail.send(src.at[xl], dst.at[x], left),
    ]

    def finish():
        mail.recv(r1)
        made.append(mail.send(relay.at[0], dst.at[xl, top], right))
        mail.recv(r2)
        made.append(mail.send(relay.at[1], dst.at[xr, low], left))
        return made

    return finish


def share_partials_kernel(o_ref, st_ref, o_out, st_out, relay, ss, rs, ls):
    x, y, k, z = coords()
    mail = Mail(ss, rs)
    greet([dev(m4(x + d), y, k, z) for d in (1, 2, 3)])
    made = [mail.send(st_ref, st_out.at[x], dev(m4(x + d), y, k, z)) for d in (1, 3, 2)]
    finish = exchange_x(mail, x, y, k, z, o_ref, o_out, relay)
    own = [
        pltpu.make_async_copy(o_ref.at[x], o_out.at[x], ls.at[0]),
        pltpu.make_async_copy(st_ref, st_out.at[x], ls.at[1]),
    ]
    for copy in own:
        copy.start()
    for i in finish() + made:
        mail.recv(i)
    for copy in own:
        copy.wait()
    mail.close()


def share_partials(o, st):
    return comm_call(
        share_partials_kernel, "share_partials", 3, 12,
        [((4, 192, 384), BF), ((4, 8, 1536), F32)],
        [pltpu.VMEM((2, 96, 384), BF)],
        [o, st],
    )


def reduce_attention_kernel(
    dq_ref, dkv_ref, br_ref, dq_out, dkv_out, br_out,
    relay_x, relay_y, mate_in, summed, far_in, z_in, z_sum, ss, rs, ls,
):
    x, y, k, z = coords()
    mail = Mail(ss, rs)
    up, down = dev(x, m4(y + 1), k, z), dev(x, m4(y + 3), k, z)
    mate = dev(x, y, 1 - k, z)
    greet(
        [dev(m4(x + 1), y, k, z), dev(m4(x + 3), y, k, z), up, down, mate]
        + [dev(x, y, k, m4(z + d)) for d in (1, 2, 3)]
    )
    yh = lax.div(y, 2)
    far = 1 - yh
    c1 = mail.send(dkv_ref.at[far * 2 + 1 - k], mate_in.at[0], mate)
    c2 = mail.send(dkv_ref.at[yh * 2 + 1 - k], mate_in.at[1], mate)
    zs = spread_z(mail, z, x, y, k, br_ref, z_in)
    finish = exchange_x(mail, x, y, k, z, dq_ref, dq_out, relay_x)
    own = pltpu.make_async_copy(dq_ref.at[x], dq_out.at[x], ls.at[0])
    own.start()
    mail.recv(c1)
    summed[...] = (dkv_ref[far * 2 + k].astype(F32) + mate_in[0].astype(F32)).astype(BF)
    top, low = pl.ds(0, 192), pl.ds(192, 192)
    y1 = mail.send(summed.at[top], relay_y.at[0], up)
    y2 = mail.send(summed.at[low], relay_y.at[1], down)
    mail.recv(c2)
    dkv_out[...] = dkv_ref[yh * 2 + k].astype(F32) + mate_in[1].astype(F32)
    for i in zs:
        mail.recv(i)
    total = br_ref[z].astype(F32)
    for d in (1, 2, 3):
        total = total + z_in[m4(z + d)].astype(F32)
    z_sum[...] = total.astype(BF)
    made = [mail.send(z_sum, br_out.at[z], dev(x, y, k, m4(z + d))) for d in (1, 3, 2)]
    own_z = pltpu.make_async_copy(z_sum, br_out.at[z], ls.at[1])
    own_z.start()
    mail.recv(y1)
    y3 = mail.send(relay_y.at[0], far_in.at[top], up)
    mail.recv(y2)
    y4 = mail.send(relay_y.at[1], far_in.at[low], down)
    made += finish()
    mail.recv(y3)
    mail.recv(y4)
    dkv_out[...] += far_in[...].astype(F32)
    for i in made:
        mail.recv(i)
    own.wait()
    own_z.wait()
    mail.close()


def reduce_attention(dq, dkv, br):
    return comm_call(
        reduce_attention_kernel, "reduce_attention", 4, 24,
        [((4, 192, 384), BF), ((384, 384), F32), ((4, 96, 768), BF)],
        [
            pltpu.VMEM((2, 96, 384), BF),
            pltpu.VMEM((2, 192, 384), BF),
            pltpu.VMEM((2, 384, 384), BF),
            pltpu.VMEM((384, 384), BF),
            pltpu.VMEM((384, 384), BF),
            pltpu.VMEM((4, 96, 768), BF),
            pltpu.VMEM((96, 768), BF),
        ],
        [dq, dkv, br],
        [False, True, True],
        [False, True, False],
    )


GCOLS = 2304
GHALF = 1152


def reduce_weights_kernel(
    g_ref, n1_ref, w_out, n1_out,
    mate_in, e, relay1, fwd1, in1, f, relay2, fwd2, in2, ss, rs, ls,
):
    x, y, k, z = coords()
    mail = Mail(ss, rs)
    mate = dev(x, y, 1 - k, z)
    step = [
        (dev(m4(x + 1), y, k, z), dev(m4(x + 3), y, k, z)),
        (dev(x, m4(y + 1), k, z), dev(x, m4(y + 3), k, z)),
    ]
    greet(list(step[0] + step[1]) + [mate] + [dev(x, y, k, m4(z + d)) for d in (1, 2, 3)])
    cs = []
    for n in range(2):
        cs.append(mail.send(g_ref.at[1 - k, n], mate_in.at[n], mate))
    zs = spread_z(mail, z, x, y, k, n1_ref, n1_out)
    own = pltpu.make_async_copy(n1_ref.at[z], n1_out.at[z], ls.at[0])
    own.start()
    pos = (x, y)
    r1 = []
    plain = []
    for n in range(2):
        a = pos[n]
        mail.recv(cs[n])

        def add(i, _):
            e[n, i] = (g_ref[k, n, i].astype(F32) + mate_in[n, i].astype(F32)).astype(BF)
            return 0

        lax.fori_loop(0, 4, add, 0)
        opp = m4(a + 2)
        r1.append(
            (
                mail.send(e.at[n, opp, pl.ds(0, 2)], relay1.at[n, 0], step[n][0]),
                mail.send(e.at[n, opp, pl.ds(2, 2)], relay1.at[n, 1], step[n][1]),
            )
        )
        plain.append(
            (
                mail.send(e.at[n, m4(a + 1), pl.ds(2, 2)], in1.at[n, 0, pl.ds(2, 2)], step[n][0]),
                mail.send(e.at[n, m4(a + 3), pl.ds(0, 2)], in1.at[n, 1, pl.ds(0, 2)], step[n][1]),
            )
        )
    more = []
    for n in range(2):
        a = pos[n]
        mail.recv(r1[n][0])
        fwd1[n, 0] = (
            e[n, m4(a + 1), pl.ds(0, 2)].astype(F32) + relay1[n, 0].astype(F32)
        ).astype(BF)
        m1 = mail.send(fwd1.at[n, 0], in1.at[n, 0, pl.ds(0, 2)], step[n][0])
        mail.recv(r1[n][1])
        fwd1[n, 1] = (
            e[n, m4(a + 3), pl.ds(2, 2)].astype(F32) + relay1[n, 1].astype(F32)
        ).astype(BF)
        m2 = mail.send(fwd1.at[n, 1], in1.at[n, 1, pl.ds(2, 2)], step[n][1])
        more.append((m1, m2))
    r2 = []
    plain2 = []
    c0, c1 = pl.ds(0, 640), pl.ds(640, 512)
    for n in range(2):
        a, b = pos[n], pos[1 - n]
        for i in plain[n] + more[n]:
            mail.recv(i)
        f[n] = (
            e[n, a].astype(F32) + in1[n, 0].astype(F32) + in1[n, 1].astype(F32)
        ).astype(BF)
        go = step[1 - n]
        r2.append(
            (
                mail.send(f.at[n, m4(b + 2), :, c0], relay2.at[n, :, c0], go[0]),
                mail.send(f.at[n, m4(b + 2), :, c1], relay2.at[n, :, c1], go[1]),
            )
        )
        plain2.append(
            (
                mail.send(f.at[n, m4(b + 1), :, c1], in2.at[n, 0, :, c1], go[0]),
                mail.send(f.at[n, m4(b + 3), :, c0], in2.at[n, 1, :, c0], go[1]),
            )
        )
    more2 = []
    for n in range(2):
        b = pos[1 - n]
        go = step[1 - n]
        mail.recv(r2[n][0])
        fwd2[n, :, c0] = (
            f[n, m4(b + 1), :, c0].astype(F32) + relay2[n, :, c0].astype(F32)
        ).astype(BF)
        m1 = mail.send(fwd2.at[n, :, c0], in2.at[n, 0, :, c0], go[0])
        mail.recv(r2[n][1])
        fwd2[n, :, c1] = (
            f[n, m4(b + 3), :, c1].astype(F32) + relay2[n, :, c1].astype(F32)
        ).astype(BF)
        m2 = mail.send(fwd2.at[n, :, c1], in2.at[n, 1, :, c1], go[1])
        more2.append((m1, m2))
    for n in range(2):
        b = pos[1 - n]
        for i in plain2[n] + more2[n]:
            mail.recv(i)
        w_out[n] = f[n, b].astype(F32) + in2[n, 0].astype(F32) + in2[n, 1].astype(F32)
    for i in zs:
        mail.recv(i)
    own.wait()
    mail.close()


def reduce_weights(g, n1):
    def buf(*lead):
        return pltpu.VMEM(lead + (24, GHALF), BF)

    return comm_call(
        reduce_weights_kernel, "reduce_weights", 5, 29,
        [((2, 24, GHALF), F32), ((4, 96, 768), BF)],
        [
            buf(2, 4, 4), buf(2, 4, 4), buf(2, 2, 2), buf(2, 2, 2), buf(2, 2, 4),
            buf(2, 4), buf(2), buf(2), buf(2, 2),
        ],
        [g, n1],
        [True, False],
        [True, False],
    )


def finish_kernel(p_ref, v_ref, p_out, v_out, cin, xin, yin, zin, t1, t2, t3, ss, rs, ls):
    x, y, k, z = coords()
    mail = Mail(ss, rs)
    mate = dev(x, y, 1 - k, z)
    xs = [dev(m4(x + d), y, k, z) for d in (1, 3, 2)]
    ys = [dev(x, m4(y + d), k, z) for d in (1, 3, 2)]
    zs = [dev(x, y, k, m4(z + d)) for d in (1, 3, 2)]
    greet([mate] + xs + ys + zs)
    c = mail.send(v_ref, cin, mate)
    ps = [mail.send(p_ref, p_out.at[z], d) for d in zs]
    own = pltpu.make_async_copy(p_ref, p_out.at[z], ls.at[0])
    own.start()
    mail.recv(c)
    t1[...] = v_ref[...] + cin[...]

    def stage(mine, slots, me, peers):
        made = [mail.send(mine, slots.at[me], d) for d in peers]
        slots[me] = mine[...]
        for i in made:
            mail.recv(i)
        return (slots[0] + slots[1]) + (slots[2] + slots[3])

    t2[...] = stage(t1, xin, x, xs)
    full = stage(t2, yin, y, ys)
    t3[...] = full[0:32]
    v_out[pl.ds(32, 16)] = full[32:48]
    v_out[pl.ds(0, 32)] = stage(t3, zin, z, zs)
    for i in ps:
        mail.recv(i)
    own.wait()
    mail.close()


def finish(p, v):
    return comm_call(
        finish_kernel, "finish", 6, 16,
        [((4, 96, 768), BF), ((48, 128), F32)],
        [
            pltpu.VMEM((48, 128), F32),
            pltpu.VMEM((4, 48, 128), F32),
            pltpu.VMEM((4, 48, 128), F32),
            pltpu.VMEM((4, 32, 128), F32),
            pltpu.VMEM((48, 128), F32),
            pltpu.VMEM((48, 128), F32),
            pltpu.VMEM((32, 128), F32),
        ],
        [p, v],
        [False, True],
        [False, True],
    )


NT = (((1,), (1,)), ((), ()))


def attention_forward_kernel(a_ref, kv_ref, kpos_ref, qpos_ref, o_ref, st_ref, kvt):
    lane = lax.broadcasted_iota(jnp.int32, (384, 128), 1)
    for h in range(3):
        cols = slice(128 * h, 128 * h + 128)
        kvt[...] = kv_ref[:, cols].T

        def tile(j, _):
            a = a_ref[j, :, cols]
            aq = jnp.where(lane < 64, a, jnp.zeros_like(a))
            s = lax.dot_general(kv_ref[:, cols], aq, NT, preferred_element_type=F32)
            kp = kpos_ref[...]
            ok = jnp.concatenate([kp, kp, kp], axis=1) <= qpos_ref[j]
            s = jnp.where(ok, s, -1e30)
            top = jnp.max(s, axis=0, keepdims=True)
            p = jnp.exp(s - top)
            total = jnp.sum(p, axis=0, keepdims=True)
            o = jnp.dot(kvt[...], p.astype(BF), preferred_element_type=F32)[64:128]
            o = o / total
            gt = a.astype(F32).T[64:128]
            o_ref[j, 64 * h : 64 * h + 64, :] = o.astype(BF)
            st_ref[j, h : h + 1, :] = top + jnp.log(total)
            st_ref[j, 4 + h : 5 + h, :] = jnp.sum(o * gt, axis=0, keepdims=True)
            return 0

        lax.fori_loop(0, 4, tile, 0)
    st_ref[:, 3:4, :] = jnp.zeros((4, 1, 384), F32)
    st_ref[:, 7:8, :] = jnp.zeros((4, 1, 384), F32)


def attention_backward_kernel(
    a_ref, kv_ref, kpos_ref, qpos_ref, st_ref, dq_ref, dkv_ref, kvt, acc_k, acc_v
):
    lane = lax.broadcasted_iota(jnp.int32, (384, 128), 1)
    wide = lax.broadcasted_iota(jnp.int32, (1536, 128), 1)
    for h in range(3):
        cols = slice(128 * h, 128 * h + 128)
        kvt[...] = kv_ref[:, cols].T
        acc_k[...] = jnp.zeros_like(acc_k)
        acc_v[...] = jnp.zeros_like(acc_v)

        def tile(j, _):
            a = a_ref[j, :, cols]
            zero = jnp.zeros_like(a)
            aq = jnp.where(lane < 64, a, zero)
            ag = jnp.where(lane < 64, zero, a)
            kv = kv_ref[:, cols]
            s = lax.dot_general(kv, aq, NT, preferred_element_type=F32)
            kp = kpos_ref[...]
            ok = jnp.concatenate([kp, kp, kp], axis=1) <= qpos_ref[j]
            p = jnp.where(ok, jnp.exp(s - st_ref[j, h : h + 1, :]), 0.0)
            gp = lax.dot_general(kv, ag, NT, preferred_element_type=F32)
            gs = (p * (gp - st_ref[j, 4 + h : 5 + h, :])).astype(BF)
            acc_v[...] += jnp.dot(p.astype(BF), a, preferred_element_type=F32)
            acc_k[...] += jnp.dot(gs, a, preferred_element_type=F32)
            dq = jnp.dot(kvt[...], gs, preferred_element_type=F32)[0:64]
            dq_ref[j, 64 * h : 64 * h + 64, :] = (dq * 0.125).astype(BF)
            return 0

        lax.fori_loop(0, 4, tile, 0)
        dkv_ref[:, cols] = jnp.where(wide < 64, acc_k[...], acc_v[...]).astype(BF)


def local_call(kernel, name, outs, scratch, args):
    vspec = pl.BlockSpec(memory_space=pltpu.VMEM)
    return pl.pallas_call(
        kernel,
        name=name,
        out_shape=[jax.ShapeDtypeStruct(*o) for o in outs],
        in_specs=[vspec] * len(args),
        out_specs=[vspec] * len(outs),
        scratch_shapes=scratch,
        compiler_params=pltpu.CompilerParams(vmem_limit_bytes=60 * 1024 * 1024),
    )(*args)


def gelu_parts(pre_act):
    cdf_val = 0.5 * (1.0 + jax.scipy.special.erf(pre_act * 0.7071067811865476))
    pdf_val = jnp.exp(-0.5 * pre_act * pre_act) * 0.3989422804014327
    return cdf_val + pre_act * pdf_val


def dot(spec, a, b):
    return jnp.einsum(spec, a, b, preferred_element_type=F32)


def rotate(t, cosine, sine):
    half = ROT // 2
    first, second = t[..., :half], t[..., half:ROT]
    cb, sb = cosine[:, None, :], sine[:, None, :]
    return jnp.concatenate(
        [first * cb - second * sb, second * cb + first * sb, t[..., ROT:]], axis=-1
    )


def shards(
    layer_input_residual, positions, ln1_gain, ln1_bias, ln2_gain, ln2_bias, w_qkv,
    query_key_value_bias, w_out, b_out, w_up, up_bias_vector, w_down, b_down, grad_out,
):
    c = lax.axis_index("context")
    z = lax.axis_index("tensor")
    x_in = layer_input_residual[0]
    g_in = grad_out[0]
    vec = jnp.stack([ln1_gain, ln1_bias, ln2_gain, ln2_bias, b_out, b_down], axis=1)
    src = jnp.concatenate(
        [w_up, w_down, w_qkv.reshape(24, 576), w_out, jnp.pad(vec, ((0, 0), (0, 122)))], axis=1
    )
    whole = gather_weights(src).reshape(768, WCOLS)
    up_w, down_w = whole[:, :768], whole[:, 768:1536]
    qkv_w, out_w = whole[:, 1536:2112], whole[:, 2112:2304]
    vec_f = whole[:, 2304:2310].astype(F32)
    gain1, bias1, gain2, bias2 = vec_f[:, 0], vec_f[:, 1], vec_f[:, 2], vec_f[:, 3]
    bias_sum = vec_f[:, 4] + vec_f[:, 5]

    centered = x_in - jnp.mean(x_in, axis=-1, keepdims=True)
    rstd = lax.rsqrt(jnp.mean(centered * centered, axis=-1, keepdims=True) + norm_eps)
    xhat = centered * rstd
    n1 = (xhat * gain1 + bias1).astype(BF)
    n2 = (xhat * gain2 + bias2).astype(BF)
    gbf = g_in.astype(BF)

    proj = dot("td,dj->tj", n1, qkv_w) + query_key_value_bias.reshape(1, 576)
    pos16 = positions.reshape(4, 4, 384)
    own_pos = lax.dynamic_slice_in_dim(positions.reshape(16, 384), c, 1, 0)[0]
    freqs = jnp.exp(-(jnp.arange(8).astype(F32) * (2.0 / ROT)) * math.log(10000.0))
    angles = own_pos.astype(F32)[:, None] * freqs
    cosine, sine = jnp.cos(angles), jnp.sin(angles)
    q = rotate(proj[:, :192].reshape(384, 3, HS), cosine, sine).astype(BF) * BF(0.125)
    kk = rotate(proj[:, 192:384].reshape(384, 3, HS), cosine, sine).astype(BF)
    vv = proj[:, 384:].reshape(384, 3, HS).astype(BF)
    ga = dot("td,di->ti", gbf, out_w).astype(BF).reshape(384, 3, HS)
    a_own = jnp.concatenate([q, ga], axis=-1).reshape(384, 384)
    kv_own = jnp.concatenate([kk, vv], axis=-1).reshape(384, 384)

    pre_act = dot("td,df->tf", n2, up_w) + up_bias_vector
    act = jax.nn.gelu(pre_act, approximate=False).astype(BF)
    g_pre = dot("td,df->tf", gbf, down_w) * gelu_parts(pre_act)
    g_b_up = jnp.sum(g_pre, axis=0)
    g_pre_bf = g_pre.astype(BF)
    g_n2 = dot("tf,df->td", g_pre_bf, up_w).astype(BF).reshape(4, 96, 768)

    a_all, kv_all, n2_parts = gather_attention(a_own, kv_own, g_n2)

    qpos = lax.dynamic_slice_in_dim(pos16, lax.rem(c, 4), 1, 1)
    kpos = lax.dynamic_slice_in_dim(pos16, lax.div(c, 4), 1, 0).reshape(1536, 1)
    kpos = jnp.broadcast_to(kpos, (1536, 128))
    kv_flat = kv_all.reshape(1536, 384)
    o_part, st_part = local_call(
        attention_forward_kernel, "attention_forward",
        [((4, 192, 384), BF), ((4, 8, 384), F32)],
        [pltpu.VMEM((128, 1536), BF)],
        [a_all, kv_flat, kpos, qpos],
    )
    o_all, st_all = share_partials(o_part, st_part.transpose(1, 0, 2).reshape(8, 1536))
    lse_i, del_i = st_all[:, 0:4], st_all[:, 4:8]
    top = jnp.max(lse_i, axis=0)
    lse = top + jnp.log(jnp.sum(jnp.exp(lse_i - top), axis=0))
    share = jnp.exp(lse_i - lse)
    delta = jnp.sum(share * del_i, axis=0)
    st = jnp.concatenate([lse, delta], axis=0).reshape(8, 4, 384).transpose(1, 0, 2)
    own_share = lax.dynamic_slice_in_dim(share, lax.div(c, 4) * 384, 384, 2)[:, :3]
    attended = (
        jnp.sum(own_share[:, :, None, :] * o_all.reshape(4, 3, 64, 384).astype(F32), axis=0)
        .astype(BF)
        .reshape(192, 384)
    )
    branch = dot("it,di->td", attended, out_w) + dot("tf,df->td", act, down_w)
    branch = branch.astype(BF).reshape(4, 96, 768)

    dq_part, dkv_part = local_call(
        attention_backward_kernel, "attention_backward",
        [((4, 192, 384), BF), ((1536, 384), BF)],
        [pltpu.VMEM((128, 1536), BF), pltpu.VMEM((1536, 128), F32), pltpu.VMEM((1536, 128), F32)],
        [a_all, kv_flat, kpos, qpos, st],
    )
    dq_all, dkv, br_all = reduce_attention(dq_part, dkv_part.reshape(4, 384, 384), branch)
    layer_out = x_in + br_all.reshape(384, 768).astype(F32) + bias_sum

    dq = jnp.sum(dq_all.astype(F32), axis=0).T.reshape(384, 3, HS)
    dkv = dkv.reshape(384, 3, 2, HS)
    g_q = rotate(dq, cosine, -sine).reshape(384, 192)
    g_k = rotate(dkv[:, :, 0], cosine, -sine).reshape(384, 192)
    g_v = dkv[:, :, 1].reshape(384, 192)
    g_proj = jnp.concatenate([g_q, g_k, g_v], axis=1)
    g_b_qkv = jnp.sum(g_proj, axis=0)
    g_proj_bf = g_proj.astype(BF)
    g_n1 = dot("tj,dj->td", g_proj_bf, qkv_w).astype(BF).reshape(4, 96, 768)

    grads = jnp.concatenate(
        [
            dot("td,tf->df", n2, g_pre_bf).astype(BF),
            dot("td,tf->df", gbf, act).astype(BF),
            dot("td,tj->dj", n1, g_proj_bf).astype(BF),
            dot("td,it->di", gbf, attended).astype(BF),
        ],
        axis=1,
    )
    grads = grads.reshape(2, 4, 2, 2, 24, 2, GHALF)
    along_x = grads[..., 0, :].transpose(3, 1, 2, 0, 4, 5).reshape(2, 4, 4, 24, GHALF)
    along_y = grads[..., 1, :].transpose(3, 2, 0, 1, 4, 5).reshape(2, 4, 4, 24, GHALF)
    own_w, n1_parts = reduce_weights(jnp.stack([along_x, along_y], axis=1), g_n1)
    own_w = jnp.concatenate([own_w[0], own_w[1]], axis=1)

    s1 = jnp.sum(n1_parts.astype(F32), axis=0)
    s2 = jnp.sum(n2_parts.astype(F32), axis=0)
    xh = lax.dynamic_slice_in_dim(xhat, z * 96, 96, 0)
    rs = lax.dynamic_slice_in_dim(rstd, z * 96, 96, 0)
    go = lax.dynamic_slice_in_dim(g_in, z * 96, 96, 0)

    def norm_back(g, gain):
        u = g * gain
        return rs * (
            u
            - jnp.mean(u, axis=-1, keepdims=True)
            - xh * jnp.mean(u * xh, axis=-1, keepdims=True)
        )

    piece = (norm_back(s1, gain1) + norm_back(s2, gain2)).astype(BF)
    sums = jnp.stack(
        [
            jnp.sum(s1 * xh, axis=0), jnp.sum(s1, axis=0),
            jnp.sum(s2 * xh, axis=0), jnp.sum(s2, axis=0), jnp.sum(go, axis=0),
        ]
    )
    small = jnp.concatenate(
        [
            jnp.pad(sums.reshape(30, 128), ((0, 2), (0, 0))),
            jnp.pad(jnp.concatenate([g_b_qkv, g_b_up]), (0, 704)).reshape(16, 128),
        ]
    )
    rows, small = finish(piece, small)
    grad_in = g_in + rows.reshape(384, 768).astype(F32)
    mine = lax.axis_index("shard") * 16 + c
    own_vec = lax.dynamic_slice_in_dim(small[:30].reshape(5, 768), mine * 24, 24, 1)
    biases = small[32:48].reshape(2048)
    return (
        layer_out[None], grad_in[None],
        own_vec[0], own_vec[1], own_vec[2], own_vec[3],
        own_w[:, 1536:2112].reshape(24, 3, 192),
        biases[:576].reshape(3, 192),
        own_w[:, 2112:2304],
        own_vec[4],
        own_w[:, :768],
        biases[576:1344],
        own_w[:, 768:1536],
        own_vec[4],
    )


def solution(mesh):
    rows = P(("shard", "context"))
    token = P("shard", "context", None)
    wide = P(("shard", "context"), "tensor")
    qkv = P(("shard", "context"), None, "tensor")
    in_specs = (
        token, P("shard", None), rows, rows, rows, rows, qkv, P(None, "tensor"),
        wide, rows, wide, P("tensor"), wide, rows, token,
    )
    out_specs = (
        token, token, rows, rows, rows, rows, qkv, P(None, "tensor"),
        wide, rows, wide, P("tensor"), wide, rows,
    )
    return jax.shard_map(shards, mesh=mesh, in_specs=in_specs, out_specs=out_specs, check_vma=False)
```

```python
import functools
import math

import jax
import jax.numpy as jnp
from jax import lax
from jax.experimental import pallas as pl
from jax.experimental.pallas import tpu as pltpu
from jax.sharding import PartitionSpec as P

HS = 64
ROT = 16
BF = jnp.bfloat16
F32 = jnp.float32
MESH = pl.DeviceIdType.MESH
norm_eps = 1e-05


def coords():
    s = lax.axis_index("shard")
    c = lax.axis_index("context")
    z = lax.axis_index("tensor")
    x = lax.div(c, 4)
    yh = lax.rem(lax.div(c, 2), 2)
    k = lax.rem(c, 2)
    return x, yh * 2 + s, k, z


def dev(x, y, k, z):
    return (lax.rem(y, 2), x * 4 + lax.div(y, 2) * 2 + k, z)


def m4(a):
    return lax.rem(a, 4)


class Mail:
    def __init__(self, send_sems, recv_sems):
        self.send_sems, self.recv_sems, self.made = send_sems, recv_sems, []

    def send(self, src, dst, device):
        i = len(self.made)
        assert i < self.send_sems.shape[0]
        copy = pltpu.make_async_remote_copy(
            src_ref=src,
            dst_ref=dst,
            send_sem=self.send_sems.at[i],
            recv_sem=self.recv_sems.at[i],
            device_id=device,
            device_id_type=MESH,
        )
        copy.start()
        self.made.append(copy)
        return i

    def recv(self, i):
        self.made[i].wait_recv()

    def close(self):
        for copy in self.made:
            copy.wait_send()


def greet(devices):
    barrier = pltpu.get_barrier_semaphore()
    for device in devices:
        pl.semaphore_signal(barrier, inc=1, device_id=device, device_id_type=MESH)
    pl.semaphore_wait(barrier, len(devices))


class Bounce:
    def __init__(self, src, via, dst, sem_in, sem_out):
        self.first = pltpu.make_async_copy(src, via, sem_in)
        self.last = pltpu.make_async_copy(via, dst, sem_out)
        self.first.start()

    def turn(self):
        self.first.wait()
        self.last.start()

    def wait(self):
        self.last.wait()


def comm_call(kernel, name, cid, n_copies, outs, scratch, args, in_vmem=None, out_vmem=None):
    anyspec = pl.BlockSpec(memory_space=pl.ANY)
    vspec = pl.BlockSpec(memory_space=pltpu.VMEM)
    in_vmem = in_vmem or [False] * len(args)
    out_vmem = out_vmem or [False] * len(outs)
    return pl.pallas_call(
        kernel,
        name=name,
        out_shape=[jax.ShapeDtypeStruct(*o) for o in outs],
        in_specs=[vspec if v else anyspec for v in in_vmem],
        out_specs=[vspec if v else anyspec for v in out_vmem],
        scratch_shapes=list(scratch)
        + [
            pltpu.SemaphoreType.DMA((n_copies,)),
            pltpu.SemaphoreType.DMA((n_copies,)),
            pltpu.SemaphoreType.DMA((6,)),
        ],
        compiler_params=pltpu.CompilerParams(
            collective_id=cid, has_side_effects=True, vmem_limit_bytes=56 * 1024 * 1024
        ),
    )(*args)


WCOLS = 2432
P_CUT = (0, 640, 1280)
Q_CUT = (1280, 1792, 2432)


def gather_weights_kernel(src, out, via, ss, rs, ls):
    x, y, k, z = coords()
    mail = Mail(ss, rs)

    def row(xx, yy):
        return lax.rem(yy, 2) * 16 + xx * 4 + lax.div(yy, 2) * 2 + k

    xs = [x, m4(x + 3), m4(x + 1), m4(x + 2)]
    ys = [y, m4(y + 3), m4(y + 1), m4(y + 2)]
    mate = dev(x, y, 1 - k, z)
    step = {
        "x": (dev(xs[2], y, k, z), dev(xs[1], y, k, z)),
        "y": (dev(x, ys[2], k, z), dev(x, ys[1], k, z)),
    }
    greet([step["x"][0], step["x"][1], step["y"][0], step["y"][1], mate])
    me = row(x, y)
    own = Bounce(src, via, out.at[me], ls.at[0], ls.at[1])

    def part(r, lo, hi):
        return out.at[r, :, pl.ds(lo, hi - lo)]

    def begin(view, r, cut, axis):
        return [
            mail.send(view, part(r, cut[0], cut[2]), step[axis][0]),
            mail.send(view, part(r, cut[0], cut[2]), step[axis][1]),
        ]

    def own_view(cut):
        return src.at[:, pl.ds(cut[0], cut[2] - cut[0])]

    mates = []

    def to_mate(r, lo, hi):
        mates.append(mail.send(part(r, lo, hi), part(r, lo, hi), mate))

    plans = [("x", "y", P_CUT), ("y", "x", Q_CUT)]
    first = [begin(own_view(cut), me, cut, a) for a, b, cut in plans]
    second = [[begin(own_view(cut), me, cut, b)] for a, b, cut in plans]
    mates.append(mail.send(src, out.at[me], mate))

    def at(a, i, j):
        return row(xs[i], ys[j]) if a == "x" else row(xs[j], ys[i])

    own.turn()
    relays = [[], []]
    for i in (1, 2):
        for n, (a, b, cut) in enumerate(plans):
            mail.recv(first[n][i - 1])
            r = at(a, i, 0)
            lo, hi = (cut[0], cut[1]) if i == 1 else (cut[1], cut[2])
            relays[n].append(mail.send(part(r, lo, hi), part(r, lo, hi), step[a][i - 1]))
            second[n].append(begin(part(r, cut[0], cut[2]), r, cut, b))
            to_mate(r, cut[0], cut[2])
    for n, (a, b, cut) in enumerate(plans):
        for i in relays[n]:
            mail.recv(i)
        r = at(a, 3, 0)
        second[n].append(begin(part(r, cut[0], cut[2]), r, cut, b))
        to_mate(r, cut[0], cut[2])
    late = []
    for i in range(4):
        for n, (a, b, cut) in enumerate(plans):
            pair = []
            for j in (1, 2):
                mail.recv(second[n][i][j - 1])
                r = at(a, i, j)
                lo, hi = (cut[0], cut[1]) if j == 1 else (cut[1], cut[2])
                pair.append(mail.send(part(r, lo, hi), part(r, lo, hi), step[b][j - 1]))
                to_mate(r, cut[0], cut[2])
            late.append((pair, at(a, i, 3), cut))
    for pair, r, cut in late:
        for i in pair:
            mail.recv(i)
        to_mate(r, cut[0], cut[2])
    for i in mates:
        mail.recv(i)
    own.wait()
    mail.close()


def gather_weights(src):
    return comm_call(
        gather_weights_kernel, "gather_weights", 1, 80,
        [((32, 24, WCOLS), BF)], [pltpu.VMEM((24, WCOLS), BF)], [src],
    )[0]


def spread_z(mail, z, x, y, k, src, dst):
    made = []
    for d in (1, 3, 2):
        peer = m4(z + d)
        made.append(mail.send(src.at[peer], dst.at[z], dev(x, y, k, peer)))
    return made


def gather_attention_kernel(a_ref, kv_ref, n2_ref, a_out, kv_out, n2_out, relay, via_a, via_kv, via_n, ss, rs, ls):
    x, y, k, z = coords()
    mail = Mail(ss, rs)
    xl, xr = m4(x + 3), m4(x + 1)
    right, left = dev(xr, y, k, z), dev(xl, y, k, z)
    up, down = dev(x, m4(y + 1), k, z), dev(x, m4(y + 3), k, z)
    mate = dev(x, y, 1 - k, z)
    greet([right, left, up, down, mate] + [dev(x, y, k, m4(z + d)) for d in (1, 2, 3)])
    slot = lax.div(y, 2) * 2 + k
    far = (1 - lax.div(y, 2)) * 2 + k
    top, low = pl.ds(0, 192), pl.ds(192, 192)
    y1 = mail.send(kv_ref.at[top], relay.at[0], up)
    y2 = mail.send(kv_ref.at[low], relay.at[1], down)
    x1 = mail.send(a_ref, a_out.at[x], right)
    x2 = mail.send(a_ref, a_out.at[x], left)
    c1 = mail.send(kv_ref, kv_out.at[slot], mate)
    zs = spread_z(mail, z, x, y, k, n2_ref, n2_out)
    locals_ = [
        Bounce(a_ref, via_a, a_out.at[x], ls.at[0], ls.at[1]),
        Bounce(kv_ref, via_kv, kv_out.at[slot], ls.at[2], ls.at[3]),
        Bounce(n2_ref.at[z], via_n, n2_out.at[z], ls.at[4], ls.at[5]),
    ]
    for copy in locals_:
        copy.turn()
    up_slot = lax.div(m4(y + 3), 2) * 2 + k
    down_slot = lax.div(m4(y + 1), 2) * 2 + k
    mail.recv(y1)
    y3 = mail.send(relay.at[0], kv_out.at[up_slot, top], up)
    mail.recv(y2)
    y4 = mail.send(relay.at[1], kv_out.at[down_slot, low], down)
    mail.recv(x1)
    x3 = mail.send(a_out.at[xl, top], a_out.at[xl, top], right)
    mail.recv(x2)
    x4 = mail.send(a_out.at[xr, low], a_out.at[xr, low], left)
    mail.recv(y3)
    mail.recv(y4)
    c2 = mail.send(kv_out.at[far], kv_out.at[far], mate)
    for i in [x3, x4, c1, c2] + zs:
        mail.recv(i)
    for copy in locals_:
        copy.wait()
    mail.close()


def gather_attention(a, kv, n2):
    return comm_call(
        gather_attention_kernel, "gather_attention", 2, 16,
        [((4, 384, 384), BF), ((4, 384, 384), BF), ((4, 96, 768), BF)],
        [
            pltpu.VMEM((2, 192, 384), BF),
            pltpu.VMEM((384, 384), BF),
            pltpu.VMEM((384, 384), BF),
            pltpu.VMEM((96, 768), BF),
        ],
        [a, kv, n2],
    )


def exchange_x(mail, x, y, k, z, src, dst, relay):
    xl, xr, xo = m4(x + 3), m4(x + 1), m4(x + 2)
    right, left = dev(xr, y, k, z), dev(xl, y, k, z)
    top, low = pl.ds(0, 96), pl.ds(96, 96)
    r1 = mail.send(src.at[xo, top], relay.at[0], right)
    r2 = mail.send(src.at[xo, low], relay.at[1], left)
    made = [
        mail.send(src.at[xr], dst.at[x], right),
        mail.send(src.at[xl], dst.at[x], left),
    ]

    def finish():
        mail.recv(r1)
        made.append(mail.send(relay.at[0], dst.at[xl, top], right))
        mail.recv(r2)
        made.append(mail.send(relay.at[1], dst.at[xr, low], left))
        return made

    return finish


def share_partials_kernel(o_ref, st_ref, o_out, st_out, relay, via_o, via_st, ss, rs, ls):
    x, y, k, z = coords()
    mail = Mail(ss, rs)
    greet([dev(m4(x + d), y, k, z) for d in (1, 2, 3)])
    made = [mail.send(st_ref, st_out.at[x], dev(m4(x + d), y, k, z)) for d in (1, 3, 2)]
    finish = exchange_x(mail, x, y, k, z, o_ref, o_out, relay)
    own = [
        Bounce(o_ref.at[x], via_o, o_out.at[x], ls.at[0], ls.at[1]),
        Bounce(st_ref, via_st, st_out.at[x], ls.at[2], ls.at[3]),
    ]
    for copy in own:
        copy.turn()
    for i in finish() + made:
        mail.recv(i)
    for copy in own:
        copy.wait()
    mail.close()


def share_partials(o, st):
    return comm_call(
        share_partials_kernel, "share_partials", 3, 12,
        [((4, 192, 384), BF), ((4, 4, 8, 384), F32)],
        [
            pltpu.VMEM((2, 96, 384), BF),
            pltpu.VMEM((192, 384), BF),
            pltpu.VMEM((4, 8, 384), F32),
        ],
        [o, st],
    )


def reduce_attention_kernel(
    dq_ref, dkv_ref, br_ref, dq_out, dkv_out, br_out,
    relay_x, relay_y, mate_in, summed, far_in, z_in, z_sum, via, ss, rs, ls,
):
    x, y, k, z = coords()
    mail = Mail(ss, rs)
    up, down = dev(x, m4(y + 1), k, z), dev(x, m4(y + 3), k, z)
    mate = dev(x, y, 1 - k, z)
    greet(
        [dev(m4(x + 1), y, k, z), dev(m4(x + 3), y, k, z), up, down, mate]
        + [dev(x, y, k, m4(z + d)) for d in (1, 2, 3)]
    )
    yh = lax.div(y, 2)
    far = 1 - yh
    c1 = mail.send(dkv_ref.at[far * 2 + 1 - k], mate_in.at[0], mate)
    c2 = mail.send(dkv_ref.at[yh * 2 + 1 - k], mate_in.at[1], mate)
    zs = spread_z(mail, z, x, y, k, br_ref, z_in)
    finish = exchange_x(mail, x, y, k, z, dq_ref, dq_out, relay_x)
    own = Bounce(dq_ref.at[x], via, dq_out.at[x], ls.at[0], ls.at[2])
    mail.recv(c1)
    summed[...] = (dkv_ref[far * 2 + k].astype(F32) + mate_in[0].astype(F32)).astype(BF)
    top, low = pl.ds(0, 192), pl.ds(192, 192)
    y1 = mail.send(summed.at[top], relay_y.at[0], up)
    y2 = mail.send(summed.at[low], relay_y.at[1], down)
    own.turn()
    mail.recv(c2)
    dkv_out[...] = dkv_ref[yh * 2 + k].astype(F32) + mate_in[1].astype(F32)
    for i in zs:
        mail.recv(i)
    total = br_ref[z].astype(F32)
    for d in (1, 2, 3):
        total = total + z_in[m4(z + d)].astype(F32)
    z_sum[...] = total.astype(BF)
    made = [mail.send(z_sum, br_out.at[z], dev(x, y, k, m4(z + d))) for d in (1, 3, 2)]
    own_z = pltpu.make_async_copy(z_sum, br_out.at[z], ls.at[1])
    own_z.start()
    mail.recv(y1)
    y3 = mail.send(relay_y.at[0], far_in.at[top], up)
    mail.recv(y2)
    y4 = mail.send(relay_y.at[1], far_in.at[low], down)
    made += finish()
    mail.recv(y3)
    mail.recv(y4)
    dkv_out[...] += far_in[...].astype(F32)
    for i in made:
        mail.recv(i)
    own.wait()
    own_z.wait()
    mail.close()


def reduce_attention(dq, dkv, br):
    return comm_call(
        reduce_attention_kernel, "reduce_attention", 4, 24,
        [((4, 192, 384), BF), ((384, 384), F32), ((4, 96, 768), BF)],
        [
            pltpu.VMEM((2, 96, 384), BF),
            pltpu.VMEM((2, 192, 384), BF),
            pltpu.VMEM((2, 384, 384), BF),
            pltpu.VMEM((384, 384), BF),
            pltpu.VMEM((384, 384), BF),
            pltpu.VMEM((4, 96, 768), BF),
            pltpu.VMEM((96, 768), BF),
            pltpu.VMEM((192, 384), BF),
        ],
        [dq, dkv, br],
        [False, True, True],
        [False, True, False],
    )


GCOLS = 2304
GHALF = 1152


def reduce_weights_kernel(
    g_ref, n1_ref, n2_ref, x_ref, rows_ref, v_ref, w_out, p_out, v_out,
    mate_in, e, relay1, fwd1, in1, f, relay2, fwd2, in2,
    n1_in, n1_own, x_own, piece, cin, xin, yin, zin, t1, t2, t3, ss, rs, ls,
):
    x, y, k, z = coords()
    mail = Mail(ss, rs)
    mate = dev(x, y, 1 - k, z)
    step = [
        (dev(m4(x + 1), y, k, z), dev(m4(x + 3), y, k, z)),
        (dev(x, m4(y + 1), k, z), dev(x, m4(y + 3), k, z)),
    ]
    x_peers = [step[0][0], step[0][1], dev(m4(x + 2), y, k, z)]
    y_peers = [step[1][0], step[1][1], dev(x, m4(y + 2), k, z)]
    z_peers = [dev(x, y, k, m4(z + d)) for d in (1, 3, 2)]
    greet([mate] + x_peers + y_peers + z_peers)
    cv = mail.send(v_ref, cin, mate)
    cs = [mail.send(g_ref.at[1 - k, n], mate_in.at[n], mate) for n in range(2)]
    zs = spread_z(mail, z, x, y, k, n1_ref, n1_in)
    own = [
        pltpu.make_async_copy(n1_ref.at[z], n1_own, ls.at[0]),
        pltpu.make_async_copy(x_ref.at[z], x_own, ls.at[1]),
    ]
    for copy in own:
        copy.start()

    def spread(mine, slots, me, peers):
        slots[me] = mine[...]
        return [mail.send(mine, slots.at[me], d) for d in peers]

    def gathered(slots, made):
        for i in made:
            mail.recv(i)
        return (slots[0] + slots[1]) + (slots[2] + slots[3])

    mail.recv(cv)
    t1[...] = v_ref[...] + cin[...]
    vx = spread(t1, xin, x, x_peers)
    pos = (x, y)
    r1 = []
    plain = []
    for n in range(2):
        a = pos[n]
        mail.recv(cs[n])

        def add(i, _):
            e[n, i] = (g_ref[k, n, i].astype(F32) + mate_in[n, i].astype(F32)).astype(BF)
            return 0

        lax.fori_loop(0, 4, add, 0)
        opp = m4(a + 2)
        r1.append(
            (
                mail.send(e.at[n, opp, pl.ds(0, 2)], relay1.at[n, 0], step[n][0]),
                mail.send(e.at[n, opp, pl.ds(2, 2)], relay1.at[n, 1], step[n][1]),
            )
        )
        plain.append(
            (
                mail.send(e.at[n, m4(a + 1), pl.ds(2, 2)], in1.at[n, 0, pl.ds(2, 2)], step[n][0]),
                mail.send(e.at[n, m4(a + 3), pl.ds(0, 2)], in1.at[n, 1, pl.ds(0, 2)], step[n][1]),
            )
        )
    t2[...] = gathered(xin, vx)
    vy = spread(t2, yin, y, y_peers)
    more = []
    for n in range(2):
        a = pos[n]
        mail.recv(r1[n][0])
        fwd1[n, 0] = (
            e[n, m4(a + 1), pl.ds(0, 2)].astype(F32) + relay1[n, 0].astype(F32)
        ).astype(BF)
        m1 = mail.send(fwd1.at[n, 0], in1.at[n, 0, pl.ds(0, 2)], step[n][0])
        mail.recv(r1[n][1])
        fwd1[n, 1] = (
            e[n, m4(a + 3), pl.ds(2, 2)].astype(F32) + relay1[n, 1].astype(F32)
        ).astype(BF)
        m2 = mail.send(fwd1.at[n, 1], in1.at[n, 1, pl.ds(2, 2)], step[n][1])
        more.append((m1, m2))
    for copy in own:
        copy.wait()
    for i in zs:
        mail.recv(i)
    s1 = n1_own[...].astype(F32)
    for d in (1, 2, 3):
        s1 = s1 + n1_in[m4(z + d)].astype(F32)
    s2 = n2_ref[0].astype(F32)
    for d in (1, 2, 3):
        s2 = s2 + n2_ref[d].astype(F32)
    xhat, rstd = standardize(x_own[...])
    back = norm_back(s1 * rows_ref[4:5], xhat, rstd) + norm_back(s2 * rows_ref[5:6], xhat, rstd)
    piece[...] = back.astype(BF)
    ps = [mail.send(piece, p_out.at[z], d) for d in z_peers]
    own_p = pltpu.make_async_copy(piece, p_out.at[z], ls.at[2])
    own_p.start()
    full = gathered(yin, vy)
    t3[...] = full[0:32]
    v_out[pl.ds(32, 16)] = full[32:48]
    vz = spread(t3, zin, z, z_peers)
    r2 = []
    plain2 = []
    c0, c1 = pl.ds(0, 640), pl.ds(640, 512)
    for n in range(2):
        a, b = pos[n], pos[1 - n]
        for i in plain[n] + more[n]:
            mail.recv(i)
        f[n] = (
            e[n, a].astype(F32) + in1[n, 0].astype(F32) + in1[n, 1].astype(F32)
        ).astype(BF)
        go = step[1 - n]
        r2.append(
            (
                mail.send(f.at[n, m4(b + 2), :, c0], relay2.at[n, :, c0], go[0]),
                mail.send(f.at[n, m4(b + 2), :, c1], relay2.at[n, :, c1], go[1]),
            )
        )
        plain2.append(
            (
                mail.send(f.at[n, m4(b + 1), :, c1], in2.at[n, 0, :, c1], go[0]),
                mail.send(f.at[n, m4(b + 3), :, c0], in2.at[n, 1, :, c0], go[1]),
            )
        )
    v_out[pl.ds(0, 32)] = gathered(zin, vz)
    more2 = []
    for n in range(2):
        b = pos[1 - n]
        go = step[1 - n]
        mail.recv(r2[n][0])
        fwd2[n, :, c0] = (
            f[n, m4(b + 1), :, c0].astype(F32) + relay2[n, :, c0].astype(F32)
        ).astype(BF)
        m1 = mail.send(fwd2.at[n, :, c0], in2.at[n, 0, :, c0], go[0])
        mail.recv(r2[n][1])
        fwd2[n, :, c1] = (
            f[n, m4(b + 3), :, c1].astype(F32) + relay2[n, :, c1].astype(F32)
        ).astype(BF)
        m2 = mail.send(fwd2.at[n, :, c1], in2.at[n, 1, :, c1], go[1])
        more2.append((m1, m2))
    for n in range(2):
        b = pos[1 - n]
        for i in plain2[n] + more2[n]:
            mail.recv(i)
        w_out[:, n * GHALF : (n + 1) * GHALF] = (
            f[n, b].astype(F32) + in2[n, 0].astype(F32) + in2[n, 1].astype(F32)
        )
    for i in ps:
        mail.recv(i)
    own_p.wait()
    mail.close()


def reduce_weights(g, n1, n2, x_rows, rows, v):
    def buf(*lead):
        return pltpu.VMEM(lead + (24, GHALF), BF)

    return comm_call(
        reduce_weights_kernel, "reduce_weights", 5, 44,
        [((24, GCOLS), F32), ((4, 96, 768), BF), ((48, 128), F32)],
        [
            buf(2, 4, 4), buf(2, 4, 4), buf(2, 2, 2), buf(2, 2, 2), buf(2, 2, 4),
            buf(2, 4), buf(2), buf(2), buf(2, 2),
            pltpu.VMEM((4, 96, 768), BF),
            pltpu.VMEM((96, 768), BF),
            pltpu.VMEM((96, 768), F32),
            pltpu.VMEM((96, 768), BF),
            pltpu.VMEM((48, 128), F32),
            pltpu.VMEM((4, 48, 128), F32),
            pltpu.VMEM((4, 48, 128), F32),
            pltpu.VMEM((4, 32, 128), F32),
            pltpu.VMEM((48, 128), F32),
            pltpu.VMEM((48, 128), F32),
            pltpu.VMEM((32, 128), F32),
        ],
        [g, n1, n2, x_rows, rows, v],
        [True, False, True, False, True, True],
        [True, False, True],
    )


def standardize(t):
    centered = t - jnp.mean(t, axis=-1, keepdims=True)
    rstd = lax.rsqrt(jnp.mean(centered * centered, axis=-1, keepdims=True) + norm_eps)
    return centered * rstd, rstd


def norm_back(u, xhat, rstd):
    return rstd * (
        u - jnp.mean(u, axis=-1, keepdims=True) - xhat * jnp.mean(u * xhat, axis=-1, keepdims=True)
    )


NN = (((1,), (0,)), ((), ()))
NT = (((1,), (1,)), ((), ()))
TN = (((0,), (0,)), ((), ()))
HEADS_HERE = (slice(0, 128), slice(128, 256), slice(256, 384))


def mm(a, b, dims):
    return lax.dot_general(a, b, dims, preferred_element_type=F32)


def low_half(shape):
    return lax.rem(lax.broadcasted_iota(jnp.int32, shape, 1), 128) < 64


def turn_head(t, tables_ref, sign):
    return (
        t * tables_ref[0]
        + sign * (pltpu.roll(t, 120, 1) * tables_ref[1] + pltpu.roll(t, 8, 1) * tables_ref[2])
    )


def pre_kernel(
    x_ref, g_ref, w_ref, bias_ref, upb_ref, tab_ref,
    n1_ref, n2_ref, gb_ref, a_ref, kv_ref, act_ref, gp_ref, gn_ref, rows_ref,
):
    vec = w_ref[:, 2304:2432].astype(F32).T
    xhat, _ = standardize(x_ref[...])
    n1_ref[...] = (xhat * vec[0:1] + vec[1:2]).astype(BF)
    n2_ref[...] = (xhat * vec[2:3] + vec[3:4]).astype(BF)
    grad = g_ref[...]
    gb_ref[...] = grad.astype(BF)
    qa = mm(n1_ref[...], w_ref[:, 1536:1920], NN) + bias_ref[0:1]
    ga = mm(gb_ref[...], w_ref[:, 1536:1920], NN)
    kv = mm(n1_ref[...], w_ref[:, 1920:2304], NN) + bias_ref[1:2]
    low = low_half((384, 128))
    for cols in HEADS_HERE:
        q = turn_head(qa[:, cols], tab_ref, 1.0).astype(BF).astype(F32) * 0.125
        a_ref[:, cols] = jnp.where(low, q, ga[:, cols]).astype(BF)
        kv_ref[:, cols] = turn_head(kv[:, cols], tab_ref, 1.0).astype(BF)
    pre = mm(n2_ref[...], w_ref[:, 0:768], NN) + upb_ref[...]
    cdf = 0.5 * (1.0 + lax.erf(pre * 0.7071067811865476))
    pdf = jnp.exp(-0.5 * pre * pre) * 0.3989422804014327
    act_ref[...] = (pre * cdf).astype(BF)
    gp = mm(gb_ref[...], w_ref[:, 768:1536], NN) * (cdf + pre * pdf)
    gp_ref[...] = gp.astype(BF)
    gn = mm(gp_ref[...], w_ref[:, 0:768], NT)
    gn_ref[...] = gn.astype(BF)
    rows_ref[0:1] = jnp.sum(gn * xhat, axis=0, keepdims=True)
    rows_ref[1:2] = jnp.sum(gn, axis=0, keepdims=True)
    rows_ref[2:3] = jnp.sum(grad, axis=0, keepdims=True) * 0.25
    rows_ref[3:4] = jnp.sum(gp, axis=0, keepdims=True)
    rows_ref[4:5] = vec[0:1]
    rows_ref[5:6] = vec[2:3]
    rows_ref[6:7] = vec[4:5] + vec[5:6]
    rows_ref[7:8] = jnp.zeros((1, 768), F32)


def spread_key_positions(pos_ref, kpos):
    x = lax.div(lax.axis_index("context"), 4)
    for m in range(4):
        kpos[384 * m : 384 * m + 384] = jnp.broadcast_to(pos_ref[x, m], (128, 384)).T


def allowed(kpos, pos_ref, j):
    kp = kpos[...]
    mine = lax.rem(lax.axis_index("context"), 4)
    return jnp.concatenate([kp, kp, kp], axis=1) <= pos_ref[j, mine]


def attention_forward_kernel(a_ref, kv_ref, pos_ref, o_ref, st_ref, kvt, kpos):
    spread_key_positions(pos_ref, kpos)
    low = low_half((384, 128))
    for h, cols in enumerate(HEADS_HERE):
        kvt[...] = kv_ref[:, cols].T

        def tile(j, _):
            a = a_ref[j, :, cols]
            aq = jnp.where(low, a, jnp.zeros_like(a))
            s = mm(kv_ref[:, cols], aq, NT)
            s = jnp.where(allowed(kpos, pos_ref, j), s, -1e30)
            top = jnp.max(s, axis=0, keepdims=True)
            p = jnp.exp(s - top)
            total = jnp.sum(p, axis=0, keepdims=True)
            o = mm(kvt[...], p.astype(BF), NN)[64:128]
            o = o / total
            gt = a.astype(F32).T[64:128]
            o_ref[j, 64 * h : 64 * h + 64, :] = o.astype(BF)
            st_ref[j, h : h + 1, :] = top + jnp.log(total)
            st_ref[j, 4 + h : 5 + h, :] = jnp.sum(o * gt, axis=0, keepdims=True)
            return 0

        lax.fori_loop(0, 4, tile, 0)
    st_ref[:, 3:4, :] = jnp.zeros((4, 1, 384), F32)
    st_ref[:, 7:8, :] = jnp.zeros((4, 1, 384), F32)


def attention_backward_kernel(
    a_ref, kv_ref, pos_ref, sts_ref, os_ref, act_ref, wd_ref, wa_ref,
    dq_ref, dkv_ref, att_ref, br_ref, kvt, kpos, acc_k, acc_v, st, wide_att,
):
    spread_key_positions(pos_ref, kpos)
    x = lax.div(lax.axis_index("context"), 4)
    parts = sts_ref[:, :, 0:4, :]
    top = jnp.max(parts, axis=0)
    norm = top + jnp.log(jnp.sum(jnp.exp(parts - top), axis=0))
    st[:, 0:4, :] = norm
    st[:, 4:8, :] = jnp.sum(jnp.exp(parts - norm) * sts_ref[:, :, 4:8, :], axis=0)
    share = jnp.exp(sts_ref[:, x, 0:4, :] - st[x, 0:4, :])
    for h in range(3):
        rows = slice(64 * h, 64 * h + 64)
        att = share[0, h : h + 1] * os_ref[0, rows].astype(F32)
        for i in (1, 2, 3):
            att = att + share[i, h : h + 1] * os_ref[i, rows].astype(F32)
        att_ref[rows] = att.astype(BF)
        wide_att[128 * h : 128 * h + 64] = jnp.zeros((64, 384), F32)
        wide_att[128 * h + 64 : 128 * h + 128] = att
    br_ref[...] = (
        mm(wide_att[...].T.astype(BF), wa_ref[...], NT) + mm(act_ref[...], wd_ref[...], NT)
    ).astype(BF)
    low = low_half((384, 128))
    for h, cols in enumerate(HEADS_HERE):
        kvt[...] = kv_ref[:, cols].T
        acc_k[...] = jnp.zeros_like(acc_k)
        acc_v[...] = jnp.zeros_like(acc_v)

        def tile(j, _):
            a = a_ref[j, :, cols]
            zero = jnp.zeros_like(a)
            kv = kv_ref[:, cols]
            s = mm(kv, jnp.where(low, a, zero), NT)
            p = jnp.where(allowed(kpos, pos_ref, j), jnp.exp(s - st[j, h : h + 1, :]), 0.0)
            gp = mm(kv, jnp.where(low, zero, a), NT)
            gs = (p * (gp - st[j, 4 + h : 5 + h, :])).astype(BF)
            acc_v[...] += mm(p.astype(BF), a, NN)
            acc_k[...] += mm(gs, a, NN)
            dq = mm(kvt[...], gs, NN)[0:64]
            dq_ref[j, 64 * h : 64 * h + 64, :] = (dq * 0.125).astype(BF)
            return 0

        lax.fori_loop(0, 4, tile, 0)
        dkv_ref[:, cols] = jnp.where(low_half((1536, 128)), acc_k[...], acc_v[...]).astype(BF)


def post_kernel(
    dq_ref, dkv_ref, att_ref, n1_ref, n2_ref, gb_ref, act_ref, gp_ref, w_ref, tab_ref, x_ref,
    rows_ref, g_ref, gn_ref, v_ref, wide, ga, gkv, big,
):
    dq = dq_ref[0].astype(F32)
    for i in (1, 2, 3):
        dq = dq + dq_ref[i].astype(F32)
    for h in range(3):
        wide[128 * h : 128 * h + 64] = dq[64 * h : 64 * h + 64]
        wide[128 * h + 64 : 128 * h + 128] = att_ref[64 * h : 64 * h + 64].astype(F32)
    packed = wide[...].T
    v_ref[...] = jnp.zeros_like(v_ref)
    for h, cols in enumerate(HEADS_HERE):
        t = turn_head(packed[:, cols], tab_ref, -1.0)
        v_ref[38 + h : 39 + h] = jnp.sum(t, axis=0, keepdims=True)
        ga[:, cols] = t.astype(BF)
        t = turn_head(dkv_ref[:, cols], tab_ref, -1.0)
        v_ref[41 + h : 42 + h] = jnp.sum(t, axis=0, keepdims=True)
        gkv[:, cols] = t.astype(BF)
    low = low_half((384, 384))
    t = ga[...]
    zero = jnp.zeros_like(t)
    only_q, only_att = jnp.where(low, t, zero), jnp.where(low, zero, t)
    gn = mm(only_q, w_ref[:, 0:384], NT) + mm(gkv[...], w_ref[:, 384:768], NT)
    gn_ref[...] = gn.astype(BF)
    xhat, _ = standardize(x_ref[...])
    sums = [
        jnp.sum(gn * xhat, axis=0, keepdims=True), jnp.sum(gn, axis=0, keepdims=True),
        rows_ref[0:1], rows_ref[1:2], rows_ref[2:3],
    ]
    for i, row in enumerate(sums):
        for j in range(6):
            v_ref[6 * i + j : 6 * i + j + 1] = row[:, 128 * j : 128 * j + 128]
    for j in range(6):
        v_ref[32 + j : 33 + j] = rows_ref[3:4, 128 * j : 128 * j + 128]
    for part in range(2):
        if part == 0:
            big[:, 0:768] = mm(n2_ref[...], gp_ref[...], TN)
            big[:, 768:1152] = mm(gb_ref[...], act_ref[:, 0:384], TN)
        else:
            big[:, 0:384] = mm(gb_ref[...], act_ref[:, 384:768], TN)
            big[:, 384:768] = mm(n1_ref[...], only_q, TN) + mm(gb_ref[...], only_att, TN)
            big[:, 768:1152] = mm(n1_ref[...], gkv[...], TN)
        for r in range(32):
            y, xx = (r // 2) % 2 * 2 + r // 16, (r // 4) % 4
            i, j = (xx, y) if part == 0 else (y, xx)
            g_ref[r % 2, part, i, j] = big[24 * r : 24 * r + 24].astype(BF)


def local_call(kernel, name, outs, scratch, args, specs=None):
    vspec = pl.BlockSpec(memory_space=pltpu.VMEM)
    specs = specs or {}

    def whole(shape):
        return pl.BlockSpec(shape, lambda i: (0,) * len(shape), pipeline_mode=pl.Buffered(1))

    return pl.pallas_call(
        kernel,
        name=name,
        grid=(1,),
        out_shape=[jax.ShapeDtypeStruct(*o) for o in outs],
        in_specs=[specs.get(n) or whole(a.shape) for n, a in enumerate(args)],
        out_specs=[whole(o[0]) for o in outs],
        scratch_shapes=scratch,
        compiler_params=pltpu.CompilerParams(vmem_limit_bytes=60 * 1024 * 1024),
    )(*args)


def columns(width, block):
    return pl.BlockSpec((768, width), lambda i: (0, block), pipeline_mode=pl.Buffered(1))


def shards(
    layer_input_residual, positions, ln1_gain, ln1_bias, ln2_gain, ln2_bias, w_qkv,
    query_key_value_bias, w_out, b_out, w_up, up_bias_vector, w_down, b_down, grad_out,
):
    c = lax.axis_index("context")
    x_in = layer_input_residual[0]
    g_in = grad_out[0]

    def pair(a, b):
        n = a.shape[0]
        both = jnp.stack([a.reshape(n, 3, HS), b.reshape(n, 3, HS)], axis=2)
        return both.reshape(n, 384)

    vec = jnp.stack([ln1_gain, ln1_bias, ln2_gain, ln2_bias, b_out, b_down], axis=1)
    src = jnp.concatenate(
        [
            w_up, w_down, pair(w_qkv[:, 0], w_out), pair(w_qkv[:, 1], w_qkv[:, 2]),
            jnp.pad(vec, ((0, 0), (0, 122))),
        ],
        axis=1,
    )
    whole = gather_weights(src).reshape(768, WCOLS)
    qb = query_key_value_bias
    bias = jnp.concatenate(
        [pair(qb[0:1], jnp.zeros_like(qb[0:1])), pair(qb[1:2], qb[2:3])], axis=0
    )
    own_pos = lax.dynamic_slice_in_dim(positions.reshape(16, 384), c, 1, 0)[0]
    lane = jnp.arange(128)
    freqs = jnp.exp(-(lax.rem(lane, 8).astype(F32) * (2.0 / ROT)) * math.log(10000.0))
    angles = own_pos.astype(F32)[:, None] * freqs
    sine = jnp.sin(angles)
    tables = jnp.stack(
        [
            jnp.where(lane < 16, jnp.cos(angles), 1.0),
            jnp.where(lane < 8, -sine, 0.0),
            jnp.where((lane >= 8) & (lane < 16), sine, 0.0),
        ]
    )
    pos_f = positions.astype(F32).reshape(4, 4, 1, 384)

    tok, sq = ((384, 768), BF), ((384, 384), BF)
    n1, n2, gb, a_own, kv_own, act, gp, g_n2, rows = local_call(
        pre_kernel, "pre",
        [tok, tok, tok, sq, sq, tok, tok, tok, ((8, 768), F32)], [],
        [x_in, g_in, whole, bias, up_bias_vector.reshape(1, 768), tables],
    )
    a_all, kv_all, n2_parts = gather_attention(a_own, kv_own, g_n2.reshape(4, 96, 768))
    kv_flat = kv_all.reshape(1536, 384)
    keys_t = [pltpu.VMEM((128, 1536), BF), pltpu.VMEM((1536, 128), F32)]
    o_part, st_part = local_call(
        attention_forward_kernel, "attention_forward",
        [((4, 192, 384), BF), ((4, 8, 384), F32)], keys_t, [a_all, kv_flat, pos_f],
    )
    o_all, st_all = share_partials(o_part, st_part)
    acc = pltpu.VMEM((1536, 128), F32)
    dq_part, dkv_part, attended, branch = local_call(
        attention_backward_kernel, "attention_backward",
        [((4, 192, 384), BF), ((1536, 384), BF), ((192, 384), BF), tok],
        keys_t + [acc, acc, pltpu.VMEM((4, 8, 384), F32), pltpu.VMEM((384, 384), F32)],
        [a_all, kv_flat, pos_f, st_all, o_all, act, whole, whole],
        {6: columns(768, 1), 7: columns(384, 4)},
    )
    dq_all, dkv, br_all = reduce_attention(
        dq_part, dkv_part.reshape(4, 384, 384), branch.reshape(4, 96, 768)
    )
    layer_out = x_in + br_all.reshape(384, 768).astype(F32) + rows[6]
    grads, g_n1, small = local_call(
        post_kernel, "post",
        [((2, 2, 4, 4, 24, GHALF), BF), tok, ((48, 128), F32)],
        [
            pltpu.VMEM((384, 384), F32), pltpu.VMEM((384, 384), BF),
            pltpu.VMEM((384, 384), BF), pltpu.VMEM((768, GHALF), F32),
        ],
        [dq_all, dkv, attended, n1, n2, gb, act, gp, whole, tables, x_in, rows],
        {8: columns(768, 2)},
    )
    own_w, pieces, small = reduce_weights(
        grads, g_n1.reshape(4, 96, 768), n2_parts, x_in.reshape(4, 96, 768), rows, small
    )
    grad_in = g_in + pieces.reshape(384, 768).astype(F32)
    mine = lax.axis_index("shard") * 16 + c
    own_vec = lax.dynamic_slice_in_dim(small[:30].reshape(5, 768), mine * 24, 24, 1)
    own_a = own_w[:, 1536:1920].reshape(24, 3, 2, HS)
    own_kv = own_w[:, 1920:2304].reshape(24, 3, 2, HS)
    own_qkv = jnp.stack(
        [t.reshape(24, 192) for t in (own_a[:, :, 0], own_kv[:, :, 0], own_kv[:, :, 1])], axis=1
    )
    b_a, b_kv = small[38:41].reshape(3, 2, HS), small[41:44].reshape(3, 2, HS)
    g_b_qkv = jnp.stack([t.reshape(192) for t in (b_a[:, 0], b_kv[:, 0], b_kv[:, 1])])
    return (
        layer_out[None], grad_in[None],
        own_vec[0], own_vec[1], own_vec[2], own_vec[3],
        own_qkv, g_b_qkv,
        own_a[:, :, 1].reshape(24, 192),
        own_vec[4],
        own_w[:, :768],
        small[32:38].reshape(768),
        own_w[:, 768:1536],
        own_vec[4],
    )


def solution(mesh):
    rows = P(("shard", "context"))
    token = P("shard", "context", None)
    wide = P(("shard", "context"), "tensor")
    qkv = P(("shard", "context"), None, "tensor")
    in_specs = (
        token, P("shard", None), rows, rows, rows, rows, qkv, P(None, "tensor"),
        wide, rows, wide, P("tensor"), wide, rows, token,
    )
    out_specs = (
        token, token, rows, rows, rows, rows, qkv, P(None, "tensor"),
        wide, rows, wide, P("tensor"), wide, rows,
    )
    return jax.shard_map(shards, mesh=mesh, in_specs=in_specs, out_specs=out_specs, check_vma=False)
```
